32 devices in a mesh: sect: 2 (over y), op: 16 (over z, x, core).
Axes of the slice: x: 2, y: 2, z: 4, core: 2. Of those that a mesh axis runs over, the one named last changes fastest.
Arguments:
- wave: bfloat16 [2, 8192, 256], P('sect', 'op'), may hold values from -6 to 6
- left_ops: bfloat16 [2, 48, 8, 256, 256], P('sect', 'op'), may hold values from -0.5 to 0.5
- right_ops: bfloat16 [2, 48, 8, 256, 256], P('sect', 'op'), may hold values from -0.375 to 0.375
- site_ops: float32 [2, 48, 4, 4], P('sect', 'op'), may hold values from -0.4375 to 0.4375
- reach: int32 [2, 48], P('sect', 'op'), may hold values from 1 to 8
- pairing: int32 [2, 8], P('sect'), may hold values from 0 to 7, each once within a row
- site_tensor: bfloat16 [2, 8, 4, 256, 256], P('sect'), may hold values from -0.25 to 0.25
Outputs:
- first_image: bfloat16 [2, 8192, 256], P('sect', 'op')
- second_image: bfloat16 [2, 8192, 256], P('sect', 'op')
- moved_image: bfloat16 [2, 8192, 256], P('sect', 'op')
The draws below stay inside these ranges and needn't reach their ends.
Inputs may be any that keep to these rules, and one draw needn't show every extreme that they name: Each term couples the sectors 0 to reach - 1. `pairing`: each row is a permutation of the 8 sectors.
All inputs are finite; a program needn't handle non-finite values.
Results may differ from the reference program's by a relative error of at most 0.008.
Values may be sent and summed in bfloat16 or wider, within the bound.
A program may use at most 128 MiB of HBM per device.

```python
import jax
import jax.numpy as jnp
from jax import lax

SECTORS = 8
BLOCK = 256
LOCAL = 4
SECTIONS = 2
TERMS = 48
ROWS = 8192


def plant(result, own_key, least, top_value):
    dims = result.shape
    index_at = [jax.random.randint(jax.random.fold_in(own_key, axis), (), 0, dims[axis]) for axis in range(len(dims))]
    result = result.at[tuple(index_at)].set(least)
    longest = dims.index(max(dims))
    index_at[longest] = (index_at[longest] + 1) % dims[longest]
    return result.at[tuple(index_at)].set(top_value)


def with_spikes(entries, key, source, target, parts, factor):
    def block_of(position):
        return (jnp.arange(entries.shape[position]) // (entries.shape[position] // parts)).reshape((-1,) + (1,) * (entries.ndim - 1 - position))

    one_side = jax.random.permutation(key, parts)[block_of(target)]
    far = (block_of(target) + parts // 2) % parts
    return jnp.where((block_of(source) == one_side) | (block_of(source) == far), factor * entries, entries)


def block_levels(key, shape, shards, smallest, top_value):
    def one(axis_at, parts):
        heights = jax.random.uniform(jax.random.fold_in(jax.random.fold_in(key, 6), axis_at), (parts,), jnp.float32, smallest / len(shards), top_value / len(shards))
        return jnp.repeat(jnp.exp(heights), shape[axis_at] // parts).reshape((-1,) + (1,) * (len(shape) - axis_at - 1))

    factor_of = one(*shards[0])
    for cut in shards[1:]:
        factor_of = factor_of * one(*cut)
    return factor_of


def scatter_about(key, extent, deviation, most, cuts=(), kind=jnp.bfloat16):
    array = deviation * jax.random.normal(key, extent, jnp.float32)
    if cuts:
        array = array * block_levels(key, extent, cuts, -0.22, 0.18)
    return jnp.clip(array, -most, most).astype(kind)


def heavy_noise(stream_key, extent, deviation, most, cuts, heavy, kind=jnp.bfloat16):
    values = deviation * jax.random.normal(stream_key, extent, jnp.float32)
    if cuts:
        values = values * block_levels(stream_key, extent, cuts, -0.22, 0.18)
    return jnp.clip(with_spikes(values, jax.random.fold_in(stream_key, 3), *heavy), -most, most).astype(kind)


def setup_inputs(seed: int = 0) -> dict:
    arg_keys = jax.random.split(jax.random.key(seed), 8)
    return {
        "wave": scatter_about(arg_keys[0], (SECTIONS, ROWS, BLOCK), 1.0, 6.0, ((0, 2), (1, 16))),
        "left_ops": heavy_noise(arg_keys[1], (SECTIONS, TERMS, SECTORS, BLOCK, BLOCK), BLOCK ** -0.5, 0.5, ((0, 2), (1, 16)), (1, 3, 16, 2.0)),
        "right_ops": scatter_about(arg_keys[2], (SECTIONS, TERMS, SECTORS, BLOCK, BLOCK), BLOCK ** -0.5, 0.375, ((0, 2), (1, 16))),
        "site_ops": scatter_about(arg_keys[3], (SECTIONS, TERMS, LOCAL, LOCAL), (LOCAL * TERMS) ** -0.5, 0.4375, ((0, 2), (1, 16)), jnp.float32),
        "reach": plant(jax.random.randint(arg_keys[4], (SECTIONS, TERMS), 1, SECTORS + 1), jax.random.fold_in(arg_keys[4], 1), 1, SECTORS).astype(jnp.int32),
        "pairing": jax.vmap(lambda own: jax.random.permutation(own, SECTORS))(jax.random.split(arg_keys[5], SECTIONS)).reshape((SECTIONS, SECTORS)).astype(jnp.int32),
        "site_tensor": scatter_about(arg_keys[6], (SECTIONS, SECTORS, LOCAL, BLOCK, BLOCK), (2 * BLOCK) ** -0.5, 0.25, ((0, 2),)),
    }


def apply_terms(wave, lefts, rights, mixers, limits, pair):
    sector_ids = jnp.arange(SECTORS, dtype=jnp.int32)
    wave_f = wave.astype(jnp.float32)

    def one_term(total, term):
        left, right, mixer, limit = term
        lifted = jnp.einsum("qab,qsbc->qsac", left.astype(jnp.float32), wave_f).astype(jnp.bfloat16)
        mask = (sector_ids < limit).astype(jnp.float32)
        mixed = jnp.einsum("xy,qyac->qxac", mixer, lifted.astype(jnp.float32), precision=lax.Precision.HIGHEST)
        mixed = (mixed * mask[:, None, None, None]).astype(jnp.bfloat16)
        paired = jnp.take(right, pair, axis=0).astype(jnp.float32)
        return total + jnp.einsum("qsac,qdc->qsad", mixed.astype(jnp.float32), paired), None

    start = jnp.zeros((SECTORS, LOCAL, BLOCK, BLOCK), jnp.float32)
    total, unused = lax.scan(one_term, start, (lefts, rights, mixers, limits))
    return total.astype(jnp.bfloat16)


def renormalize(lefts, tensor, pair):
    onehot = (pair[:, None] == jnp.arange(SECTORS, dtype=jnp.int32)[None, :]).astype(jnp.float32)
    tensor_f = tensor.astype(jnp.float32)

    def one_term(carry, left):
        lifted = jnp.einsum("qab,qsbc->qsac", left.astype(jnp.float32), tensor_f).astype(jnp.bfloat16)
        reduced = jnp.einsum("qsad,qsac->qdc", tensor_f, lifted.astype(jnp.float32)).astype(jnp.bfloat16)
        placed = jnp.einsum("qj,qdc->jdc", onehot, reduced.astype(jnp.float32), precision=lax.Precision.HIGHEST)
        return carry, placed.astype(jnp.bfloat16)

    unused, renewed = lax.scan(one_term, jnp.zeros((), jnp.float32), lefts)
    return renewed


def reference(wave, left_ops, right_ops, site_ops, reach, pairing, site_tensor):
    firsts = []
    seconds = []
    renewed = []
    for section in range(SECTIONS):
        blocks = wave[section].reshape(SECTORS, LOCAL, BLOCK, BLOCK)
        first = apply_terms(blocks, left_ops[section], right_ops[section], site_ops[section], reach[section], pairing[section])
        second = apply_terms(first, left_ops[section], right_ops[section], site_ops[section], reach[section], pairing[section])
        firsts.append(first.reshape(ROWS, BLOCK))
        seconds.append(second.reshape(ROWS, BLOCK))
        renewed.append(renormalize(left_ops[section], site_tensor[section], pairing[section]))
    moved = []
    for section in range(SECTIONS):
        blocks = wave[section].reshape(SECTORS, LOCAL, BLOCK, BLOCK)
        image = apply_terms(blocks, renewed[section - 1], right_ops[section], site_ops[section], reach[section], pairing[section])
        moved.append(image.reshape(ROWS, BLOCK))
    return jnp.stack(firsts), jnp.stack(seconds), jnp.stack(moved)
```

```python
import functools

import jax
import jax.numpy as jnp
from jax import lax
from jax.experimental import pallas as pl
from jax.experimental.pallas import tpu as pltpu
from jax.sharding import PartitionSpec as P

VM = pl.BlockSpec(memory_space=pltpu.VMEM)
SUBS = 2
BIG = 64000 * 1024


class Ring:
    def __init__(self, count):
        me = lax.axis_index("op")
        self.m = count // 2
        self.half = self.m // 2
        self.core = lax.rem(me, 2)
        self.chip = lax.div(me, 2)
        odd = lax.rem(self.chip, 2)
        low = lax.div(self.chip, 2)
        self.pos = (1 - odd) * low + odd * (self.m - 1 - low)
        self.sibling = {"op": self.chip * 2 + 1 - self.core}
        self.next = [
            {"op": self.chip_at(1) * 2 + self.core},
            {"op": self.chip_at(-1) * 2 + self.core},
        ]

    def chip_at(self, offset):
        pos = lax.rem(self.pos + offset + self.m, self.m)
        upper = lax.div(pos, self.half)
        return (1 - upper) * (2 * pos) + upper * (2 * (self.m - 1 - pos) + 1)

    def barrier(self):
        sem = pltpu.get_barrier_semaphore()
        for who in (self.next[0], self.next[1], self.sibling):
            pl.semaphore_signal(sem, inc=1, device_id=who, device_id_type=pl.DeviceIdType.MESH)
        pl.semaphore_wait(sem, 3)


def push(src, dst, send, recv, who):
    copy = pltpu.make_async_remote_copy(
        src_ref=src, dst_ref=dst, send_sem=send, recv_sem=recv, device_id=who,
        device_id_type=pl.DeviceIdType.MESH,
    )
    copy.start()
    return copy


def scatter_sum(ring, streams):
    m, half = ring.m, ring.half
    order = [half]
    for dist in range(half - 1, 0, -1):
        order += [dist, -dist]
    order.append(0)
    sent = []
    sib = {}
    for slot, offset in enumerate(order):
        chunk = ring.chip_at(offset)
        for n, st in enumerate(streams):
            sib[n, offset] = push(
                st["give"].at[chunk], st["land"].at[chunk], st["sib_send"].at[slot],
                st["sib_recv"].at[slot], ring.sibling,
            )
    arrived = set()
    hops = {}

    def local(n, offset, u):
        st = streams[n]
        if (n, offset) not in arrived:
            arrived.add((n, offset))
            sib[n, offset].wait_recv()
        chunk = ring.chip_at(offset)
        rows = st["own"].shape[1] // SUBS
        cut = pl.ds(u * rows, rows)
        return st["own"][chunk, cut, :] + st["land"][chunk, cut, :].astype(jnp.float32)

    def incoming(n, d, j, u):
        hops[n, d, j, u].wait_recv()
        return streams[n]["rbuf"][d, j, u].astype(jnp.float32)

    for j in range(half):
        dist = half - j
        for n, st in enumerate(streams):
            for u in range(SUBS):
                for d in range(2):
                    if dist == half and u != d:
                        continue
                    offset = dist if (d == 0 or dist == half) else -dist
                    value = local(n, offset, u)
                    if (n, d, j - 1, u) in hops:
                        value = value + incoming(n, d, j - 1, u)
                    st["sbuf"][d, j, u] = value.astype(jnp.bfloat16)
                    hops[n, d, j, u] = push(
                        st["sbuf"].at[d, j, u], st["rbuf"].at[d, j, u],
                        st["send"].at[d, j, u], st["recv"].at[d, j, u], ring.next[d],
                    )
    for n, st in enumerate(streams):
        for u in range(SUBS):
            value = local(n, 0, u)
            for d in range(2):
                if (n, d, half - 1, u) in hops:
                    value = value + incoming(n, d, half - 1, u)
            rows = value.shape[0]
            st["out"][pl.ds(u * rows, rows), :] = value.astype(jnp.bfloat16)
    sent += list(sib.values()) + list(hops.values())
    return sent


def gather(ring, own, whole, send, recv, sib_send, sib_recv):
    half = ring.half
    rows = own.shape[0] // SUBS
    sent, sib, hops = [], [], {}

    def part(chunk, u):
        return whole.at[chunk, ring.core, pl.ds(u * rows, rows)]

    def to_sibling(src, chunk, u):
        slot = len(sib)
        sib.append(push(src, part(chunk, u), sib_send.at[slot], sib_recv.at[slot], ring.sibling))

    for s in range(half + 1):
        for u in range(SUBS):
            for d in range(2):
                chunk = ring.chip_at(-s if d == 0 else s)
                if s == 0:
                    src = own.at[pl.ds(u * rows, rows)]
                else:
                    if (d, s - 1, u) not in hops:
                        continue
                    hops[d, s - 1, u].wait_recv()
                    src = part(chunk, u)
                if s < half and (s < half - 1 or u == d):
                    hops[d, s, u] = push(
                        src, part(chunk, u), send.at[d, s, u], recv.at[d, s, u], ring.next[d]
                    )
                if s > 0 or d == 0:
                    to_sibling(src, chunk, u)
    for copy in sib:
        copy.wait_recv()
    return sib + list(hops.values())


def gather_kernel(count, own, whole, send, recv, sib_send, sib_recv, local_sem):
    ring = Ring(count)
    ring.barrier()
    keep = pltpu.make_async_copy(own, whole.at[ring.chip, ring.core], local_sem)
    keep.start()
    sent = gather(ring, own, whole, send, recv, sib_send, sib_recv)
    for copy in sent:
        copy.wait_send()
    keep.wait()


def reduce_kernel(count, streams, regather, *refs):
    refs = list(refs)
    take = lambda n: [refs.pop(0) for _ in range(n)]
    ins = take(2 * streams)
    outs = take(streams)
    whole = take(1)[0] if regather else None
    made = []
    for n in range(streams):
        land, sbuf, rbuf, send, recv, sib_send, sib_recv = take(7)
        made.append(dict(
            own=ins[2 * n], give=ins[2 * n + 1], out=outs[n], land=land, sbuf=sbuf, rbuf=rbuf,
            send=send, recv=recv, sib_send=sib_send, sib_recv=sib_recv,
        ))
    ring = Ring(count)
    ring.barrier()
    sent = scatter_sum(ring, made)
    if regather:
        send, recv, sib_send, sib_recv, local_sem = take(5)
        keep = pltpu.make_async_copy(outs[0], whole.at[ring.chip, ring.core], local_sem)
        keep.start()
        sent += gather(ring, outs[0], whole, send, recv, sib_send, sib_recv)
        keep.wait()
    for copy in sent:
        copy.wait_send()


def gather_scratch(count):
    half = count // 4
    dma = pltpu.SemaphoreType.DMA
    slots = SUBS * (2 * half)
    return [dma((2, half, SUBS)), dma((2, half, SUBS)), dma((slots,)), dma((slots,)), dma]


def all_gather(own, count, ident):
    rows, width = own.shape
    whole = pl.pallas_call(
        functools.partial(gather_kernel, count),
        out_shape=jax.ShapeDtypeStruct((count // 2, 2, rows, width), own.dtype),
        in_specs=[VM],
        out_specs=VM,
        scratch_shapes=gather_scratch(count),
        compiler_params=pltpu.CompilerParams(
            collective_id=ident, has_side_effects=True, vmem_limit_bytes=BIG
        ),
        name="gather_rows",
    )(own)
    return whole.reshape(count * rows, width)


def reduce(pairs, count, ident, regather):
    chips, rows, width = pairs[0][0].shape
    half = chips // 2
    dma = pltpu.SemaphoreType.DMA
    out_shape = [jax.ShapeDtypeStruct((rows, width), jnp.bfloat16) for _ in pairs]
    if regather:
        out_shape.append(jax.ShapeDtypeStruct((chips, 2, rows, width), jnp.bfloat16))
    scratch = []
    for _ in pairs:
        hop = (2, half, SUBS, rows // SUBS, width)
        scratch += [
            pltpu.VMEM((chips, rows, width), jnp.bfloat16),
            pltpu.VMEM(hop, jnp.bfloat16),
            pltpu.VMEM(hop, jnp.bfloat16),
            dma((2, half, SUBS)), dma((2, half, SUBS)), dma((chips,)), dma((chips,)),
        ]
    if regather:
        scratch += gather_scratch(count)
    return pl.pallas_call(
        functools.partial(reduce_kernel, count, len(pairs), regather),
        out_shape=out_shape,
        in_specs=[VM] * (2 * len(pairs)),
        out_specs=[VM] * len(out_shape),
        scratch_shapes=scratch,
        compiler_params=pltpu.CompilerParams(
            collective_id=ident, has_side_effects=True, vmem_limit_bytes=BIG
        ),
        name="reduce_rows_gather" if regather else "reduce_rows",
    )(*[ref for pair in pairs for ref in pair])


def apply_kernel(pair, limits, core, mixers, v_ref, l_ref, r_ref, own_ref, give_ref, acc):
    q = pl.program_id(0)
    terms = l_ref.shape[0]
    block = l_ref.shape[2]
    local = v_ref.shape[0] // block
    acc[...] = jnp.zeros_like(acc)
    for t in range(terms):
        @pl.when(q < limits[t])
        def _(t=t):
            left = l_ref[t, 0]
            right = r_ref[t, 0]
            lifted = [
                jnp.dot(left, v_ref[pl.ds(s * block, block), :], preferred_element_type=jnp.float32)
                .astype(jnp.bfloat16).astype(jnp.float32)
                for s in range(local)
            ]
            for x in range(local):
                mixed = mixers[t, x * local] * lifted[0]
                for y in range(1, local):
                    mixed = mixed + mixers[t, x * local + y] * lifted[y]
                rows = pl.ds(x * block, block)
                acc[rows, :] += lax.dot_general(
                    mixed.astype(jnp.bfloat16), right, (((1,), (1,)), ((), ())),
                    preferred_element_type=jnp.float32,
                )
    here = core[0]
    chips, rows, _ = own_ref.shape
    for j in range(chips):
        own_ref[j] = acc[pl.ds(pl.multiple_of((2 * j + here) * rows, rows), rows), :]
        give_ref[j] = acc[
            pl.ds(pl.multiple_of((2 * j + 1 - here) * rows, rows), rows), :
        ].astype(jnp.bfloat16)


def apply_local(whole, lefts, rights, mixers, limits, pair, core, count):
    terms, sectors, block, _ = lefts.shape
    rows_all, width = whole.shape
    height = rows_all // sectors
    chips = count // 2
    rows = rows_all // count
    each = chips // sectors
    mats = (terms, 1, block, block)
    grid_spec = pltpu.PrefetchScalarGridSpec(
        num_scalar_prefetch=4,
        grid=(sectors,),
        in_specs=[
            pl.BlockSpec((height, width), lambda q, *_: (q, 0)),
            pl.BlockSpec(mats, lambda q, *_: (0, q, 0, 0)),
            pl.BlockSpec(mats, lambda q, pair, *_: (0, pair[q], 0, 0)),
        ],
        out_specs=[pl.BlockSpec((each, rows, width), lambda q, *_: (q, 0, 0))] * 2,
        scratch_shapes=[pltpu.VMEM((height, width), jnp.float32)],
    )
    return pl.pallas_call(
        apply_kernel,
        grid_spec=grid_spec,
        out_shape=[
            jax.ShapeDtypeStruct((chips, rows, width), jnp.float32),
            jax.ShapeDtypeStruct((chips, rows, width), jnp.bfloat16),
        ],
        compiler_params=pltpu.CompilerParams(vmem_limit_bytes=BIG),
        cost_estimate=pl.CostEstimate(
            flops=4 * terms * rows_all * width * block, transcendentals=0,
            bytes_accessed=4 * lefts.size + 8 * rows_all * width,
        ),
        name="apply_terms",
    )(pair, limits, core, mixers, whole, lefts, rights)


def renew_kernel(back, l_ref, t_ref, out_ref):
    terms = l_ref.shape[0]
    local = t_ref.shape[1]
    for t in range(terms):
        total = None
        for s in range(local):
            lifted = jnp.dot(
                l_ref[t, 0], t_ref[0, s], preferred_element_type=jnp.float32
            ).astype(jnp.bfloat16)
            term = lax.dot_general(
                t_ref[0, s], lifted, (((0,), (0,)), ((), ())),
                preferred_element_type=jnp.float32,
            )
            total = term if total is None else total + term
        out_ref[t, 0] = total.astype(jnp.bfloat16)


def renew(lefts, tensor, pair):
    terms, sectors, block, _ = lefts.shape
    local = tensor.shape[1]
    ids = jnp.arange(sectors, dtype=jnp.int32)
    back = jnp.sum((pair[None, :] == ids[:, None]) * ids[None, :], axis=1).astype(jnp.int32)
    return pl.pallas_call(
        renew_kernel,
        grid_spec=pltpu.PrefetchScalarGridSpec(
            num_scalar_prefetch=1,
            grid=(sectors,),
            in_specs=[
                pl.BlockSpec((terms, 1, block, block), lambda j, back: (0, back[j], 0, 0)),
                pl.BlockSpec((1, local, block, block), lambda j, back: (back[j], 0, 0, 0)),
            ],
            out_specs=pl.BlockSpec((terms, 1, block, block), lambda j, back: (0, j, 0, 0)),
        ),
        out_shape=jax.ShapeDtypeStruct(lefts.shape, jnp.bfloat16),
        compiler_params=pltpu.CompilerParams(vmem_limit_bytes=BIG),
        cost_estimate=pl.CostEstimate(
            flops=4 * lefts.size * local * block, transcendentals=0,
            bytes_accessed=4 * lefts.size + 2 * tensor.size,
        ),
        name="renew",
    )(back, lefts, tensor)


def shards(count, wave, left_ops, right_ops, site_ops, reach, pairing, site_tensor):
    lefts, rights, limits, pair = left_ops[0], right_ops[0], reach[0], pairing[0]
    mixers = site_ops[0].reshape(site_ops.shape[1], -1)
    core = lax.rem(lax.axis_index("op"), 2).astype(jnp.int32).reshape(1)
    renewed = renew(lefts, site_tensor[0], pair)
    size = lax.axis_size("sect")
    moved_lefts = lax.ppermute(renewed, "sect", [(i, (i + 1) % size) for i in range(size)])
    whole = all_gather(wave[0], count, 0)
    part = apply_local(whole, lefts, rights, mixers, limits, pair, core, count)
    first_own, first_full = reduce([part], count, 1, True)
    first_full = first_full.reshape(whole.shape)
    moved_part = apply_local(whole, moved_lefts, rights, mixers, limits, pair, core, count)
    second_part = apply_local(first_full, lefts, rights, mixers, limits, pair, core, count)
    second_own, moved_own = reduce([second_part, moved_part], count, 2, False)
    return first_own[None], second_own[None], moved_own[None]


def solution(mesh):
    placed = (
        P("sect", "op", None),
        P("sect", "op", None, None, None),
        P("sect", "op", None, None, None),
        P("sect", "op", None, None),
        P("sect", "op"),
        P("sect", None),
        P("sect", None, None, None, None),
    )
    return jax.shard_map(
        functools.partial(shards, mesh.shape["op"]),
        mesh=mesh,
        in_specs=placed,
        out_specs=(P("sect", "op", None), P("sect", "op", None), P("sect", "op", None)),
        check_vma=False,
    )
```

```python
import functools

import jax
import jax.numpy as jnp
from jax import lax
from jax.experimental import pallas as pl
from jax.experimental.pallas import tpu as pltpu
from jax.sharding import PartitionSpec as P

VM = pl.BlockSpec(memory_space=pltpu.VMEM)
SUBS = 2
BIG = 64000 * 1024


class Ring:
    def __init__(self, count):
        me = lax.axis_index("op")
        self.m = count // 2
        self.half = self.m // 2
        self.core = lax.rem(me, 2)
        self.chip = lax.div(me, 2)
        odd = lax.rem(self.chip, 2)
        low = lax.div(self.chip, 2)
        self.pos = (1 - odd) * low + odd * (self.m - 1 - low)
        self.sibling = {"op": self.chip * 2 + 1 - self.core}
        self.next = [
            {"op": self.chip_at(1) * 2 + self.core},
            {"op": self.chip_at(-1) * 2 + self.core},
        ]

    def chip_at(self, offset):
        pos = lax.rem(self.pos + offset + self.m, self.m)
        upper = lax.div(pos, self.half)
        return (1 - upper) * (2 * pos) + upper * (2 * (self.m - 1 - pos) + 1)

    def barrier(self):
        sem = pltpu.get_barrier_semaphore()
        for who in (self.next[0], self.next[1], self.sibling):
            pl.semaphore_signal(sem, inc=1, device_id=who, device_id_type=pl.DeviceIdType.MESH)
        pl.semaphore_wait(sem, 3)


def push(src, dst, send, recv, who):
    copy = pltpu.make_async_remote_copy(
        src_ref=src, dst_ref=dst, send_sem=send, recv_sem=recv, device_id=who,
        device_id_type=pl.DeviceIdType.MESH,
    )
    copy.start()
    return copy


def scatter_sum(ring, streams, hook=lambda step: None):
    m, half = ring.m, ring.half
    order = [half]
    for dist in range(half - 1, 0, -1):
        order += [dist, -dist]
    order.append(0)
    sent = []
    sib = {}
    for slot, offset in enumerate(order):
        chunk = ring.chip_at(offset)
        for n, st in enumerate(streams):
            sib[n, offset] = push(
                st["give"].at[chunk], st["land"].at[chunk], st["sib_send"].at[slot],
                st["sib_recv"].at[slot], ring.sibling,
            )
    arrived = set()
    hops = {}

    def local(n, offset, u):
        st = streams[n]
        if (n, offset) not in arrived:
            arrived.add((n, offset))
            sib[n, offset].wait_recv()
        chunk = ring.chip_at(offset)
        rows = st["own"].shape[1] // SUBS
        cut = pl.ds(u * rows, rows)
        return st["own"][chunk, cut, :] + st["land"][chunk, cut, :].astype(jnp.float32)

    def incoming(n, d, j, u):
        hops[n, d, j, u].wait_recv()
        return streams[n]["rbuf"][d, j, u].astype(jnp.float32)

    for j in range(half):
        dist = half - j
        for n, st in enumerate(streams):
            for u in range(SUBS):
                for d in range(2):
                    if dist == half and u != d:
                        continue
                    offset = dist if (d == 0 or dist == half) else -dist
                    value = local(n, offset, u)
                    if (n, d, j - 1, u) in hops:
                        value = value + incoming(n, d, j - 1, u)
                    st["sbuf"][d, j, u] = value.astype(jnp.bfloat16)
                    hops[n, d, j, u] = push(
                        st["sbuf"].at[d, j, u], st["rbuf"].at[d, j, u],
                        st["send"].at[d, j, u], st["recv"].at[d, j, u], ring.next[d],
                    )
        hook(j)
    for n, st in enumerate(streams):
        for u in range(SUBS):
            value = local(n, 0, u)
            for d in range(2):
                if (n, d, half - 1, u) in hops:
                    value = value + incoming(n, d, half - 1, u)
            rows = value.shape[0]
            st["out"][pl.ds(u * rows, rows), :] = value.astype(jnp.bfloat16)
    sent += list(sib.values()) + list(hops.values())
    return sent


def gather(ring, own, whole, send, recv, sib_send, sib_recv, hook):
    half = ring.half
    each = ring.m // whole.shape[0]
    rows = own.shape[0] // SUBS
    sib, hops = [], {}

    def part(chunk, u):
        start = (lax.rem(chunk, each) * 2 + ring.core) * own.shape[0] + u * rows
        return whole.at[lax.div(chunk, each), pl.ds(pl.multiple_of(start, rows), rows)]

    for s in range(half + 1):
        first = len(sib)
        for u in range(SUBS):
            for d in range(2):
                chunk = ring.chip_at(-s if d == 0 else s)
                if s == 0:
                    src = own.at[pl.ds(u * rows, rows)]
                else:
                    if (d, s - 1, u) not in hops:
                        continue
                    hops[d, s - 1, u].wait_recv()
                    src = part(chunk, u)
                if s < half and (s < half - 1 or u == d):
                    hops[d, s, u] = push(
                        src, part(chunk, u), send.at[d, s, u], recv.at[d, s, u], ring.next[d]
                    )
                if s > 0 or d == 0:
                    slot = len(sib)
                    sib.append(push(
                        src, part(chunk, u), sib_send.at[slot], sib_recv.at[slot], ring.sibling
                    ))

        def ready(first=first, last=len(sib)):
            for copy in sib[first:last]:
                copy.wait_recv()

        hook(s, ready)
    return sib + list(hops.values())


def keep_own(ring, own, whole, sem):
    each = ring.m // whole.shape[0]
    start = (lax.rem(ring.chip, each) * 2 + ring.core) * own.shape[0]
    keep = pltpu.make_async_copy(
        own,
        whole.at[lax.div(ring.chip, each), pl.ds(pl.multiple_of(start, own.shape[0]), own.shape[0])],
        sem,
    )
    keep.start()
    return keep


def apply_sector(ring, q, v, lefts, rights, mixers, limits, pair, acc, own, give):
    terms, _, block, _ = lefts.shape
    local = v.shape[1] // block
    for t in range(terms):
        left = lefts[t, q]
        right = rights[t, pair[q]]
        lifted = [
            jnp.dot(left, v[q, pl.ds(s * block, block), :], preferred_element_type=jnp.float32)
            .astype(jnp.bfloat16).astype(jnp.float32)
            for s in range(local)
        ]
        live = jnp.where(q < limits[t], 1.0, 0.0).astype(jnp.float32)
        for x in range(local):
            mixed = (live * mixers[t, x * local]) * lifted[0]
            for y in range(1, local):
                mixed = mixed + (live * mixers[t, x * local + y]) * lifted[y]
            rows = pl.ds(x * block, block)
            term = lax.dot_general(
                mixed.astype(jnp.bfloat16), right, (((1,), (1,)), ((), ())),
                preferred_element_type=jnp.float32,
            )
            acc[rows, :] = term if t == 0 else acc[rows, :] + term
    rows = own.shape[1]
    each = own.shape[0] // lefts.shape[1]
    for j in range(each):
        mine = pl.multiple_of((2 * j + ring.core) * rows, rows)
        other = pl.multiple_of((2 * j + 1 - ring.core) * rows, rows)
        own[q * each + j] = acc[pl.ds(mine, rows), :]
        give[q * each + j] = acc[pl.ds(other, rows), :].astype(jnp.bfloat16)


def renew_sector(j, back, lefts, tensor, out):
    terms = lefts.shape[0]
    local = tensor.shape[1]
    source = back[j]
    for t in range(terms):
        total = None
        for s in range(local):
            lifted = jnp.dot(
                lefts[t, source], tensor[source, s], preferred_element_type=jnp.float32
            ).astype(jnp.bfloat16)
            term = lax.dot_general(
                tensor[source, s], lifted, (((0,), (0,)), ((), ())),
                preferred_element_type=jnp.float32,
            )
            total = term if total is None else total + term
        out[t, j] = total.astype(jnp.bfloat16)


def while_gathering(ring, sectors, compute, extra=lambda step: None):
    def hook(s, ready):
        extra(s)
        ready()
        if ring.m != sectors:
            if s == ring.half:
                lax.fori_loop(0, sectors, lambda i, c: compute(i) or c, 0)
        elif s == 0 or s == ring.half:
            compute(ring.chip_at(s))
        else:
            lax.fori_loop(0, 2, lambda i, c: compute(ring.chip_at(s * (1 - 2 * i))) or c, 0)

    return hook


def load_all(pairs, sems):
    copies = [pltpu.make_async_copy(a, b, sems.at[i]) for i, (a, b) in enumerate(pairs)]
    for copy in copies:
        copy.start()
    return copies


def first_kernel(
    count, pair, back, limits, mixers, wave, left_in, right_in, tensor_in,
    whole, own, give, renewed, lefts, rights, tensor, acc, loads, local_sem, *sems
):
    ring = Ring(count)
    loaded = load_all([(left_in, lefts), (tensor_in, tensor), (right_in, rights)], loads)
    keep = keep_own(ring, wave, whole, local_sem)
    ring.barrier()
    sectors = lefts.shape[1]
    per = -(-sectors // ring.half)

    def extra(s):
        if s == 0:
            for copy in loaded:
                copy.wait()
            keep.wait()
        low, high = min(s * per, sectors), min(s * per + per, sectors)
        if low < high:
            lax.fori_loop(
                low, high, lambda j, c: renew_sector(j, back, lefts, tensor, renewed) or c, 0
            )

    def compute(q):
        apply_sector(ring, q, whole, lefts, rights, mixers, limits, pair, acc, own, give)

    sent = gather(ring, wave, whole, *sems, while_gathering(ring, sectors, compute, extra))
    for copy in sent:
        copy.wait_send()


def stream_of(refs):
    return dict(zip(
        ("own", "give", "out", "land", "sbuf", "rbuf", "send", "recv", "sib_send", "sib_recv"), refs
    ))


def second_kernel(
    count, pair, limits, mixers, own1, give1, left_in, right_in,
    out, own, give, lefts, rights, whole, acc, loads, local_sem, *rest
):
    ring = Ring(count)
    loaded = load_all([(left_in, lefts), (right_in, rights)], loads)
    ring.barrier()
    sent = scatter_sum(ring, [stream_of((own1, give1, out) + rest[:7])])
    keep = keep_own(ring, out, whole, local_sem)

    def extra(s):
        if s == 0:
            for copy in loaded:
                copy.wait()
            keep.wait()

    def compute(q):
        apply_sector(ring, q, whole, lefts, rights, mixers, limits, pair, acc, own, give)

    sent += gather(ring, out, whole, *rest[7:], while_gathering(ring, lefts.shape[1], compute, extra))
    for copy in sent:
        copy.wait_send()


def third_kernel(
    count, pair, limits, mixers, own2, give2, whole_in, left_in, right_in,
    out2, out3, whole, lefts, rights, own3, give3, acc, loads, *rest
):
    ring = Ring(count)
    loaded = load_all([(left_in, lefts), (right_in, rights), (whole_in, whole)], loads)
    ring.barrier()
    sectors = lefts.shape[1]
    per = -(-sectors // ring.half)

    def hook(s):
        if s == 0:
            for copy in loaded:
                copy.wait()
        low, high = min(s * per, sectors), min(s * per + per, sectors)
        if low < high:
            def body(q, c):
                apply_sector(ring, q, whole, lefts, rights, mixers, limits, pair, acc, own3, give3)
                return c
            lax.fori_loop(low, high, body, 0)

    sent = scatter_sum(ring, [stream_of((own2, give2, out2) + rest[:7])], hook)
    sent += scatter_sum(ring, [stream_of((own3, give3, out3) + rest[7:])])
    for copy in sent:
        copy.wait_send()


def gather_scratch(count):
    half = count // 4
    dma = pltpu.SemaphoreType.DMA
    slots = SUBS * (2 * half)
    return [dma((2, half, SUBS)), dma((2, half, SUBS)), dma((slots,)), dma((slots,)), dma]


def stream_scratch(chips, rows, width):
    half = chips // 2
    dma = pltpu.SemaphoreType.DMA
    hop = (2, half, SUBS, rows // SUBS, width)
    return [
        pltpu.VMEM((chips, rows, width), jnp.bfloat16),
        pltpu.VMEM(hop, jnp.bfloat16),
        pltpu.VMEM(hop, jnp.bfloat16),
        dma((2, half, SUBS)), dma((2, half, SUBS)), dma((chips,)), dma((chips,)),
    ]


def call(kernel, count, ident, ins, outs, scratch, name):
    shapes, specs = zip(*ins)
    return pl.pallas_call(
        functools.partial(kernel, count),
        out_shape=outs,
        in_specs=specs,
        out_specs=[VM] * len(outs),
        scratch_shapes=scratch,
        compiler_params=pltpu.CompilerParams(
            collective_id=ident, has_side_effects=True, vmem_limit_bytes=BIG
        ),
        name=name,
    )(*shapes)


def shards(count, wave, left_ops, right_ops, site_ops, reach, pairing, site_tensor):
    lefts, rights, limits, pair = left_ops[0], right_ops[0], reach[0], pairing[0]
    mixers = site_ops[0].reshape(site_ops.shape[1], -1)
    own, tensor = wave[0], site_tensor[0]
    sectors, block = lefts.shape[1:3]
    ids = jnp.arange(sectors, dtype=jnp.int32)
    back = jnp.sum((pair[None, :] == ids[:, None]) * ids[None, :], axis=1).astype(jnp.int32)
    rows, width = own.shape
    chips = count // 2
    height = count * rows // sectors
    dma = pltpu.SemaphoreType.DMA
    sm = pl.BlockSpec(memory_space=pltpu.SMEM)
    anyw = pl.BlockSpec(memory_space=pl.ANY)
    bf, f32 = jnp.bfloat16, jnp.float32
    whole_shape = (sectors, height, width)
    part = [
        jax.ShapeDtypeStruct((chips, rows, width), f32),
        jax.ShapeDtypeStruct((chips, rows, width), bf),
    ]
    mine = jax.ShapeDtypeStruct((rows, width), bf)
    ops = [pltpu.VMEM(lefts.shape, bf), pltpu.VMEM(rights.shape, bf)]
    acc = pltpu.VMEM((height, width), f32)
    small = [(pair, sm), (limits, sm), (mixers, sm)]

    whole, own1, give1, renewed = call(
        first_kernel, count, 0,
        [(pair, sm), (back, sm), (limits, sm), (mixers, sm), (own, VM), (lefts, anyw),
         (rights, anyw), (tensor, anyw)],
        [jax.ShapeDtypeStruct(whole_shape, bf)] + part + [jax.ShapeDtypeStruct(lefts.shape, bf)],
        ops + [pltpu.VMEM(tensor.shape, bf), acc, dma((3,))] + gather_scratch(count)[-1:]
        + gather_scratch(count)[:-1],
        "gather_apply",
    )
    size = lax.axis_size("sect")
    moved_lefts = lax.ppermute(renewed, "sect", [(i, (i + 1) % size) for i in range(size)])
    first_own, own2, give2 = call(
        second_kernel, count, 1,
        small + [(own1, VM), (give1, VM), (lefts, anyw), (rights, anyw)],
        [mine] + part,
        ops + [pltpu.VMEM(whole_shape, bf), acc, dma((2,))] + gather_scratch(count)[-1:]
        + stream_scratch(chips, rows, width) + gather_scratch(count)[:-1],
        "reduce_gather_apply",
    )
    second_own, moved_own = call(
        third_kernel, count, 2,
        small + [(own2, VM), (give2, VM), (whole, anyw), (moved_lefts, anyw), (rights, anyw)],
        [mine, mine],
        [pltpu.VMEM(whole_shape, bf)] + ops + [pltpu.VMEM(p.shape, p.dtype) for p in part]
        + [acc, dma((3,))] + stream_scratch(chips, rows, width) * 2,
        "reduce_apply_reduce",
    )
    return first_own[None], second_own[None], moved_own[None]


def solution(mesh):
    placed = (
        P("sect", "op", None),
        P("sect", "op", None, None, None),
        P("sect", "op", None, None, None),
        P("sect", "op", None, None),
        P("sect", "op"),
        P("sect", None),
        P("sect", None, None, None, None),
    )
    return jax.shard_map(
        functools.partial(shards, mesh.shape["op"]),
        mesh=mesh,
        in_specs=placed,
        out_specs=(P("sect", "op", None), P("sect", "op", None), P("sect", "op", None)),
        check_vma=False,
    )
```

```python
import functools

import jax
import jax.numpy as jnp
from jax import lax
from jax.experimental import pallas as pl
from jax.experimental.pallas import tpu as pltpu
from jax.sharding import PartitionSpec as P

VM = pl.BlockSpec(memory_space=pltpu.VMEM)
SUBS = 2
BIG = 67043328


class Ring:
    def __init__(self, count, sections):
        me = lax.axis_index("op")
        here = lax.axis_index("sect")
        self.sections = sections
        self.ahead = {"sect": lax.rem(here + 1, sections)}
        self.behind = {"sect": lax.rem(here + sections - 1, sections)}
        self.m = count // 2
        self.half = self.m // 2
        self.core = lax.rem(me, 2)
        self.chip = lax.div(me, 2)
        odd = lax.rem(self.chip, 2)
        low = lax.div(self.chip, 2)
        self.pos = (1 - odd) * low + odd * (self.m - 1 - low)
        self.sibling = {"op": self.chip * 2 + 1 - self.core}
        self.next = [
            {"op": self.chip_at(1) * 2 + self.core},
            {"op": self.chip_at(-1) * 2 + self.core},
        ]

    def chip_at(self, offset):
        pos = lax.rem(self.pos + offset + self.m, self.m)
        upper = lax.div(pos, self.half)
        return (1 - upper) * (2 * pos) + upper * (2 * (self.m - 1 - pos) + 1)

    def barrier(self):
        sem = pltpu.get_barrier_semaphore()
        peers = [self.next[0], self.next[1], self.sibling, self.ahead]
        if self.sections > 2:
            peers.append(self.behind)
        for who in peers:
            pl.semaphore_signal(sem, inc=1, device_id=who, device_id_type=pl.DeviceIdType.MESH)
        pl.semaphore_wait(sem, len(peers))


def push(src, dst, send, recv, who):
    copy = pltpu.make_async_remote_copy(
        src_ref=src, dst_ref=dst, send_sem=send, recv_sem=recv, device_id=who,
        device_id_type=pl.DeviceIdType.MESH,
    )
    copy.start()
    return copy


def scatter_sum(ring, streams, hook=lambda step: None):
    m, half = ring.m, ring.half
    order = [half]
    for dist in range(half - 1, 0, -1):
        order += [dist, -dist]
    order.append(0)
    sent = []
    sib = {}
    for slot, offset in enumerate(order):
        chunk = ring.chip_at(offset)
        for n, st in enumerate(streams):
            sib[n, offset] = push(
                st["give"].at[chunk], st["land"].at[chunk], st["sib_send"].at[slot],
                st["sib_recv"].at[slot], ring.sibling,
            )
    arrived = set()
    hops = {}

    def local(n, offset, u):
        st = streams[n]
        if (n, offset) not in arrived:
            arrived.add((n, offset))
            sib[n, offset].wait_recv()
        chunk = ring.chip_at(offset)
        rows = st["own"].shape[1] // SUBS
        cut = pl.ds(u * rows, rows)
        return st["own"][chunk, cut, :] + st["land"][chunk, cut, :].astype(jnp.float32)

    def incoming(n, d, j, u):
        hops[n, d, j, u].wait_recv()
        return streams[n]["rbuf"][d, j, u].astype(jnp.float32)

    for j in range(half):
        dist = half - j
        for n, st in enumerate(streams):
            for u in range(SUBS):
                for d in range(2):
                    if dist == half and u != d:
                        continue
                    offset = dist if (d == 0 or dist == half) else -dist
                    value = local(n, offset, u)
                    if (n, d, j - 1, u) in hops:
                        value = value + incoming(n, d, j - 1, u)
                    st["sbuf"][d, j, u] = value.astype(jnp.bfloat16)
                    hops[n, d, j, u] = push(
                        st["sbuf"].at[d, j, u], st["rbuf"].at[d, j, u],
                        st["send"].at[d, j, u], st["recv"].at[d, j, u], ring.next[d],
                    )
        hook(j)
    for n, st in enumerate(streams):
        for u in range(SUBS):
            value = local(n, 0, u)
            for d in range(2):
                if (n, d, half - 1, u) in hops:
                    value = value + incoming(n, d, half - 1, u)
            rows = value.shape[0]
            st["out"][pl.ds(u * rows, rows), :] = value.astype(jnp.bfloat16)
    sent += list(sib.values()) + list(hops.values())
    return sent


def gather(ring, own, whole, send, recv, sib_send, sib_recv, hook):
    half = ring.half
    each = ring.m // whole.shape[0]
    rows = own.shape[0] // SUBS
    sib, hops = [], {}

    def part(chunk, u):
        start = (lax.rem(chunk, each) * 2 + ring.core) * own.shape[0] + u * rows
        return whole.at[lax.div(chunk, each), pl.ds(pl.multiple_of(start, rows), rows)]

    for s in range(half + 1):
        first = len(sib)
        for u in range(SUBS):
            for d in range(2):
                chunk = ring.chip_at(-s if d == 0 else s)
                if s == 0:
                    src = own.at[pl.ds(u * rows, rows)]
                else:
                    if (d, s - 1, u) not in hops:
                        continue
                    hops[d, s - 1, u].wait_recv()
                    src = part(chunk, u)
                if s < half and (s < half - 1 or u == d):
                    hops[d, s, u] = push(
                        src, part(chunk, u), send.at[d, s, u], recv.at[d, s, u], ring.next[d]
                    )
                if s > 0 or d == 0:
                    slot = len(sib)
                    sib.append(push(
                        src, part(chunk, u), sib_send.at[slot], sib_recv.at[slot], ring.sibling
                    ))

        def ready(first=first, last=len(sib)):
            for copy in sib[first:last]:
                copy.wait_recv()

        hook(s, ready)
    return sib + list(hops.values())


def keep_own(ring, own, whole, sem):
    each = ring.m // whole.shape[0]
    start = (lax.rem(ring.chip, each) * 2 + ring.core) * own.shape[0]
    keep = pltpu.make_async_copy(
        own,
        whole.at[lax.div(ring.chip, each), pl.ds(pl.multiple_of(start, own.shape[0]), own.shape[0])],
        sem,
    )
    keep.start()
    return keep


def apply_sector(ring, q, v, left_of, rights, mixers, limits, pair, acc, own, give):
    terms, sectors, block, _ = rights.shape
    local = v.shape[1] // block
    for t in range(terms):
        left = left_of(t, q)
        right = rights[t, pair[q]]
        lifted = [
            jnp.dot(left, v[q, pl.ds(s * block, block), :], preferred_element_type=jnp.float32)
            .astype(jnp.bfloat16).astype(jnp.float32)
            for s in range(local)
        ]
        live = jnp.where(q < limits[t], 1.0, 0.0).astype(jnp.float32)
        for x in range(local):
            mixed = (live * mixers[t, x * local]) * lifted[0]
            for y in range(1, local):
                mixed = mixed + (live * mixers[t, x * local + y]) * lifted[y]
            rows = pl.ds(x * block, block)
            term = lax.dot_general(
                mixed.astype(jnp.bfloat16), right, (((1,), (1,)), ((), ())),
                preferred_element_type=jnp.float32,
            )
            acc[rows, :] = term if t == 0 else acc[rows, :] + term
    rows = own.shape[1]
    each = own.shape[0] // sectors
    for j in range(each):
        mine = pl.multiple_of((2 * j + ring.core) * rows, rows)
        other = pl.multiple_of((2 * j + 1 - ring.core) * rows, rows)
        own[q * each + j] = acc[pl.ds(mine, rows), :]
        give[q * each + j] = acc[pl.ds(other, rows), :].astype(jnp.bfloat16)


def renew_sector(j, back, lefts, tensor, out):
    terms = lefts.shape[0]
    local = tensor.shape[1]
    source = back[j]
    for t in range(terms):
        total = None
        for s in range(local):
            lifted = jnp.dot(
                lefts[t, source], tensor[source, s], preferred_element_type=jnp.float32
            ).astype(jnp.bfloat16)
            term = lax.dot_general(
                tensor[source, s], lifted, (((0,), (0,)), ((), ())),
                preferred_element_type=jnp.float32,
            )
            total = term if total is None else total + term
        out[j, t] = total.astype(jnp.bfloat16)


def while_gathering(ring, sectors, compute, extra=lambda step: None):
    def hook(s, ready):
        extra(s)
        ready()
        if ring.m != sectors:
            if s == ring.half:
                lax.fori_loop(0, sectors, lambda i, c: compute(i) or c, 0)
        elif s == 0 or s == ring.half:
            compute(ring.chip_at(s))
        else:
            lax.fori_loop(0, 2, lambda i, c: compute(ring.chip_at(s * (1 - 2 * i))) or c, 0)

    return hook


def load_all(pairs, sems):
    copies = [pltpu.make_async_copy(a, b, sems.at[i]) for i, (a, b) in enumerate(pairs)]
    for copy in copies:
        copy.start()
    return copies


def stream_of(refs):
    return dict(zip(
        ("own", "give", "out", "land", "sbuf", "rbuf", "send", "recv", "sib_send", "sib_recv"), refs
    ))


def whole_kernel(
    count, sections, pair, back, limits, mixers, wave, left_in, right_in, tensor_in,
    out1, out2, out3,
    lefts, rights, tensor, whole, image, renewed, moved, own_a, own_b, give1, give2, give3, acc,
    loads, local_sem, ahead_send, ahead_recv, *rest
):
    ring = Ring(count, sections)
    loaded = load_all([(left_in, lefts), (tensor_in, tensor), (right_in, rights)], loads)
    keep = keep_own(ring, wave, whole, local_sem.at[0])
    ring.barrier()
    sectors = rights.shape[1]
    per = -(-sectors // ring.half)
    streams = [
        stream_of((own, give, out) + rest[7 * i:7 * i + 7])
        for i, (own, give, out) in enumerate(
            ((own_a, give1, out1), (own_b, give2, out2), (own_a, give3, out3))
        )
    ]
    gather_sems = rest[21:25], rest[25:29]
    crossing = []

    def span(s):
        return min(s * per, sectors), min(s * per + per, sectors)

    def renew_some(s):
        if s == 0:
            for copy in loaded:
                copy.wait()
            keep.wait()
        low, high = span(s)
        if low < high:
            lax.fori_loop(
                low, high, lambda j, c: renew_sector(j, back, lefts, tensor, renewed) or c, 0
            )
        for j in range(low, high):
            crossing.append(push(
                renewed.at[j], moved.at[j], ahead_send.at[j], ahead_recv.at[j], ring.ahead
            ))

    def apply_first(q):
        apply_sector(
            ring, q, whole, lambda t, q: lefts[t, q], rights, mixers, limits, pair, acc,
            own_a, give1,
        )

    def apply_second(q):
        apply_sector(
            ring, q, image, lambda t, q: lefts[t, q], rights, mixers, limits, pair, acc,
            own_b, give2,
        )

    def apply_moved(s):
        low, high = span(s)
        for j in range(low, high):
            crossing[j].wait_recv()

        def body(q, c):
            apply_sector(
                ring, q, whole, lambda t, q: moved[q, t], rights, mixers, limits, pair, acc,
                own_a, give3,
            )
            return c

        if low < high:
            lax.fori_loop(low, high, body, 0)

    sent = gather(
        ring, wave, whole, *gather_sems[0],
        while_gathering(ring, sectors, apply_first, renew_some),
    )
    sent += scatter_sum(ring, streams[:1])
    kept = keep_own(ring, out1, image, local_sem.at[1])

    def settle(s):
        if s == 0:
            kept.wait()

    sent += gather(
        ring, out1, image, *gather_sems[1],
        while_gathering(ring, sectors, apply_second, settle),
    )
    sent += scatter_sum(ring, streams[1:2], apply_moved)
    sent += scatter_sum(ring, streams[2:])
    for copy in sent + crossing:
        copy.wait_send()


def gather_scratch(count):
    half = count // 4
    dma = pltpu.SemaphoreType.DMA
    slots = SUBS * (2 * half)
    return [dma((2, half, SUBS)), dma((2, half, SUBS)), dma((slots,)), dma((slots,))]


def stream_scratch(chips, rows, width):
    half = chips // 2
    dma = pltpu.SemaphoreType.DMA
    hop = (2, half, SUBS, rows // SUBS, width)
    return [
        pltpu.VMEM((chips, rows, width), jnp.bfloat16),
        pltpu.VMEM(hop, jnp.bfloat16),
        pltpu.VMEM(hop, jnp.bfloat16),
        dma((2, half, SUBS)), dma((2, half, SUBS)), dma((chips,)), dma((chips,)),
    ]


def shards(count, sections, wave, left_ops, right_ops, site_ops, reach, pairing, site_tensor):
    lefts, rights, limits, pair = left_ops[0], right_ops[0], reach[0], pairing[0]
    mixers = site_ops[0].reshape(site_ops.shape[1], -1)
    own, tensor = wave[0], site_tensor[0]
    sectors, block = lefts.shape[1:3]
    ids = jnp.arange(sectors, dtype=jnp.int32)
    back = jnp.sum((pair[None, :] == ids[:, None]) * ids[None, :], axis=1).astype(jnp.int32)
    rows, width = own.shape
    chips = count // 2
    height = count * rows // sectors
    dma = pltpu.SemaphoreType.DMA
    sm = pl.BlockSpec(memory_space=pltpu.SMEM)
    anyw = pl.BlockSpec(memory_space=pl.ANY)
    bf, f32 = jnp.bfloat16, jnp.float32
    image = pltpu.VMEM((sectors, height, width), bf)
    total = pltpu.VMEM((chips, rows, width), f32)
    give = pltpu.VMEM((chips, rows, width), bf)
    across = pltpu.VMEM((sectors, lefts.shape[0], block, block), bf)
    mine = jax.ShapeDtypeStruct((rows, width), bf)
    outs = pl.pallas_call(
        functools.partial(whole_kernel, count, sections),
        out_shape=[mine] * 3,
        in_specs=[sm] * 4 + [VM] + [anyw] * 3,
        out_specs=[VM] * 3,
        scratch_shapes=[
            pltpu.VMEM(lefts.shape, bf), pltpu.VMEM(rights.shape, bf),
            pltpu.VMEM(tensor.shape, bf), image, image, across, across, total, total,
            give, give, give, pltpu.VMEM((height, width), f32),
            dma((3,)), dma((2,)), dma((sectors,)), dma((sectors,)),
        ] + stream_scratch(chips, rows, width) * 3 + gather_scratch(count) * 2,
        compiler_params=pltpu.CompilerParams(
            collective_id=0, has_side_effects=True, vmem_limit_bytes=BIG
        ),
        name="images",
    )(pair, back, limits, mixers, own, lefts, rights, tensor)
    return tuple(out[None] for out in outs)


def solution(mesh):
    placed = (
        P("sect", "op", None),
        P("sect", "op", None, None, None),
        P("sect", "op", None, None, None),
        P("sect", "op", None, None),
        P("sect", "op"),
        P("sect", None),
        P("sect", None, None, None, None),
    )
    return jax.shard_map(
        functools.partial(shards, mesh.shape["op"], mesh.shape["sect"]),
        mesh=mesh,
        in_specs=placed,
        out_specs=(P("sect", "op", None), P("sect", "op", None), P("sect", "op", None)),
        check_vma=False,
    )
```
